256 devices in a mesh: heads: 8 (over y_lo, x), ctx: 32 (over z, y_hi, core).
Axes of the slice: x: 4, y: 4 (y_hi: 2, y_lo: 2; y = y_hi * 2 + y_lo), z: 8, core: 2. Of those that a mesh axis runs over, the one named last changes fastest.
Arguments:
- queries: bfloat16 [12288, 8192], P('ctx', 'heads'), may hold values from -20 to 20
- keys: bfloat16 [12288, 1024], P('ctx', 'heads'), may hold values from -20 to 20
- values: bfloat16 [12288, 1024], P('ctx', 'heads'), may hold values from -6 to 6
- positions: int32 [12288], P('ctx'), may hold values from 0 to 18431, as said below
Outputs:
- attended: bfloat16 [12288, 8192], P(('ctx', 'heads'))
The draws below stay inside these ranges and needn't reach their ends.
Inputs may be any that keep to these rules, and one draw needn't show every extreme that they name: `positions`: positions start at 0 at the first token and rise by 1 or 2 from each token to the next; exactly 6144 of these steps rise by 2.
All inputs are finite; a program needn't handle non-finite values.
Results may differ from the reference program's by a relative error of at most 0.0092.
Values may be sent and summed in bfloat16 or wider, within the bound.
A program may use at most 64 MiB of HBM per device.

```python
import math
import jax
import jax.numpy as jnp
from jax import lax

QH = 64
KVH = 8
HD = 128
GROUP = 8
TOKENS = 12288


def draw_queries(key, part):
    drawn = jax.random.truncated_normal(jax.random.fold_in(key, 1), -6.0, 6.0, (TOKENS, QH * HD), jnp.float32) * 1.2
    return drawn.astype(jnp.bfloat16)


def draw_keys(key, part):
    drawn = jax.random.truncated_normal(jax.random.fold_in(key, 2), -6.0, 6.0, (TOKENS, KVH * HD), jnp.float32) * 2.0
    return drawn.astype(jnp.bfloat16)


def draw_positions(key, part):
    order_table = jax.random.permutation(jax.random.fold_in(key, 3), TOKENS - 1)
    step_table = 1 + (order_table < TOKENS // 2).astype(jnp.int32)
    rising = jnp.cumsum(step_table).astype(jnp.int32)
    return jnp.concatenate([jnp.zeros((1,), jnp.int32), rising], 0).astype(jnp.int32)


def level_of(own_key, shape, pieces, smallest, largest):
    factor_of, own = 1.0, jax.random.fold_in(own_key, 6)
    for dim, blocks in pieces:
        heights = jnp.exp(jax.random.uniform(jax.random.fold_in(own, dim), (blocks,), jnp.float32, smallest / len(pieces), largest / len(pieces)))
        factor_of = factor_of * jnp.repeat(heights, shape[dim] // blocks).reshape([-1 if axis == dim else 1 for axis in range(len(shape))])
    return factor_of


def centred(stream_key, extent, deviation, bound, split=(), kind=jnp.bfloat16):
    values = deviation * jax.random.normal(stream_key, extent, jnp.float32)
    if split:
        values = values * level_of(stream_key, extent, split, -0.22, 0.18)
    return jnp.clip(values, -bound, bound).astype(kind)


def setup_inputs(seed: int = 0) -> dict:
    key_of = jax.random.split(jax.random.key(seed), 5)
    queries = draw_queries(jax.random.fold_in(key_of[4], 71), 0)
    keys = draw_keys(jax.random.fold_in(key_of[4], 71), 0)
    values = centred(key_of[2], (TOKENS, KVH * HD), 1.0, 6.0, ((0, 32), (1, 8)))
    positions = draw_positions(jax.random.fold_in(key_of[4], 71), 0)
    return {"queries": queries, "keys": keys, "values": values, "positions": positions}


def rotary_tables(positions, head_dim):
    step_index = jnp.arange(head_dim // 2, dtype=jnp.float32)
    base_freq = jnp.power(jnp.float32(500000.0), -(2.0 * step_index / head_dim))
    wavelen = 2.0 * math.pi / base_freq
    blend_factor = (8192.0 / wavelen - 1.0) / 3.0
    middle = (1.0 - blend_factor) * base_freq / 8.0 + blend_factor * base_freq
    inv_freq = jnp.where(wavelen < 2048.0, base_freq, jnp.where(wavelen > 8192.0, base_freq / 8.0, middle))
    angles = positions.astype(jnp.float32)[:, None] * inv_freq[None, :]
    return (jnp.cos(angles), jnp.sin(angles))

def rotate(head_data, cosine, sine_table):
    halfway = head_data.shape[-1] // 2
    first_part = head_data[..., :halfway]
    second = head_data[..., halfway:]
    cos_rows = cosine[:, None, :]
    sin_rows = sine_table[:, None, :]
    return jnp.concatenate([first_part * cos_rows - second * sin_rows, second * cos_rows + first_part * sin_rows], axis=-1)

def reference(queries, keys, values, positions):
    cosine, sine_table = rotary_tables(positions, HD)
    rot_queries = rotate(queries.astype(jnp.float32).reshape(TOKENS, QH, HD), cosine, sine_table).astype(jnp.bfloat16)
    rot_keys = rotate(keys.astype(jnp.float32).reshape(TOKENS, KVH, HD), cosine, sine_table).astype(jnp.bfloat16)
    query_groups = rot_queries.reshape(TOKENS, KVH, GROUP, HD)
    value_heads = values.reshape(TOKENS, KVH, HD)
    block_rows = math.gcd(TOKENS, 512)
    count_blocks = TOKENS // block_rows
    scale_value = 1.0 / math.sqrt(HD)
    key_index = jnp.arange(TOKENS, dtype=jnp.int32)

    def per_head(head_index):
        keys_one = lax.dynamic_index_in_dim(rot_keys, head_index, 1, keepdims=False).astype(jnp.float32)
        values_one = lax.dynamic_index_in_dim(value_heads, head_index, 1, keepdims=False).astype(jnp.float32)
        queries_one = lax.dynamic_index_in_dim(query_groups, head_index, 1, keepdims=False)

        def per_block(block_index):
            block_start = (block_index * block_rows).astype(jnp.int32)
            query_block = lax.dynamic_slice_in_dim(queries_one, block_start, block_rows, 0).astype(jnp.float32)
            scores = jnp.einsum('qgd,kd->gqk', query_block, keys_one, precision=lax.Precision.HIGHEST) * scale_value
            query_index = block_start + jnp.arange(block_rows, dtype=jnp.int32)
            allowed = key_index[None, :] <= query_index[:, None]
            scores = jnp.where(allowed[None], scores, -jnp.inf)
            row_max = lax.optimization_barrier(jnp.max(scores, axis=-1, keepdims=True))
            weights = jnp.exp(scores - row_max)
            total_sum = lax.optimization_barrier(jnp.sum(weights, axis=-1))
            rounded = lax.optimization_barrier(weights.astype(jnp.bfloat16)).astype(jnp.float32)
            mixed_values = jnp.einsum('gqk,kd->qgd', rounded, values_one, precision=lax.Precision.HIGHEST)
            return mixed_values / jnp.transpose(total_sum)[:, :, None]
        return lax.map(per_block, jnp.arange(count_blocks, dtype=jnp.int32))
    result = lax.map(per_head, jnp.arange(KVH, dtype=jnp.int32))
    result = jnp.transpose(result, (1, 2, 0, 3, 4)).reshape(TOKENS, QH * HD)
    return result.astype(jnp.bfloat16)
```

```python
import functools
import math

import jax
import jax.numpy as jnp
from jax import lax
from jax.experimental import pallas as pl
from jax.experimental.pallas import tpu as pltpu
from jax.sharding import PartitionSpec as P

HD = 128
NEG_FILL = -1e30
MESH = pl.DeviceIdType.MESH
SLABS = 8
WIDE = 4
SEQ = 7


def rotary_tables(positions, head_dim):
    step_index = jnp.arange(head_dim // 2, dtype=jnp.float32)
    base_freq = jnp.power(jnp.float32(500000.0), -(2.0 * step_index / head_dim))
    wavelen = 2.0 * math.pi / base_freq
    blend_factor = (8192.0 / wavelen - 1.0) / 3.0
    middle = (1.0 - blend_factor) * base_freq / 8.0 + blend_factor * base_freq
    inv_freq = jnp.where(
        wavelen < 2048.0, base_freq, jnp.where(wavelen > 8192.0, base_freq / 8.0, middle)
    )
    angles = positions.astype(jnp.float32)[:, None] * inv_freq[None, :]
    return (jnp.cos(angles), jnp.sin(angles))


def rotate(head_data, cosine, sine_table):
    halfway = head_data.shape[-1] // 2
    first_part = head_data[..., :halfway]
    second = head_data[..., halfway:]
    cos_rows = cosine[:, None, :]
    sin_rows = sine_table[:, None, :]
    return jnp.concatenate(
        [first_part * cos_rows - second * sin_rows, second * cos_rows + first_part * sin_rows],
        axis=-1,
    )


def attend_kernel(
    heads_n,
    q_ref,
    kv_ref,
    out_ref,
    kv_all,
    q_far,
    q_two,
    acc,
    total,
    top,
    stage,
    own_sem,
    side_sem,
    recv_sem,
    up_sem,
    down_sem,
    core_sem,
    q_sem,
    out_send,
    out_recv,
):
    rows = q_ref.shape[0]
    half = q_ref.shape[1] // 2
    tiles = half // HD
    share = rows // heads_n
    scale = math.log2(math.e) / math.sqrt(HD)
    head = lax.axis_index("heads")
    rank = lax.axis_index("ctx")
    ranks = SLABS * WIDE
    z = rank // WIDE
    place = rank % WIDE
    across = (place + 2) % WIDE
    far = ranks - 1 - rank
    mate = rank + 1 - 2 * (rank % 2)
    other = z * WIDE + across
    up = (rank + WIDE) % ranks
    down = (rank + ranks - WIDE) % ranks

    barrier = pltpu.get_barrier_semaphore()
    for peer in (mate, other, up, down):
        pl.semaphore_signal(barrier, inc=1, device_id={"ctx": peer}, device_id_type=MESH)
    for hop in range(heads_n):
        peer = (head + hop) % heads_n
        pl.semaphore_signal(
            barrier, inc=1, device_id={"heads": peer, "ctx": far}, device_id_type=MESH
        )
        if hop:
            pl.semaphore_signal(
                barrier, inc=1, device_id={"heads": peer, "ctx": rank}, device_id_type=MESH
            )
    pl.semaphore_wait(barrier, 3 + 2 * heads_n)

    def send(source, slot, peer, sem):
        return pltpu.make_async_remote_copy(
            src_ref=source,
            dst_ref=kv_all.at[slot],
            send_sem=sem,
            recv_sem=recv_sem.at[slot],
            device_id={"ctx": peer},
            device_id_type=MESH,
        )

    def arrived(slot):
        send(kv_all.at[slot], slot, mate, core_sem.at[0]).wait_recv()

    def incoming(k, upward):
        odd = k % 2
        if upward:
            mine = jnp.logical_or(odd == 1, k == 0)
            dist = jnp.where(mine, jnp.where(k == 0, 1, (k + 3) // 2), k // 2)
            slab = (z + SLABS - dist) % SLABS
            onward = jnp.where(mine, dist < 4, dist < 3)
        else:
            mine = jnp.logical_and(jnp.logical_or(odd == 1, k == 0), k < 5)
            dist = jnp.where(
                k >= 5, k - 2, jnp.where(mine, jnp.where(k == 0, 1, (k + 3) // 2), k // 2)
            )
            slab = (z + dist) % SLABS
            onward = jnp.where(mine, dist < 3, dist < 4)
        return slab * WIDE + jnp.where(mine, place, across), onward

    def relay(k):
        for upward in (True, False):
            slot, onward = incoming(k, upward)
            arrived(slot)

            @pl.when(onward)
            def _():
                if upward:
                    send(kv_all.at[slot], slot, up, up_sem.at[k + 2]).start()
                else:
                    send(kv_all.at[slot], slot, down, down_sem.at[k + 2]).start()

            send(kv_all.at[slot], slot, mate, core_sem.at[2 + 2 * k + int(upward)]).start()

    send(kv_ref, rank, up, up_sem.at[0]).start()
    send(kv_ref, rank, down, down_sem.at[0]).start()
    send(kv_ref, rank, other, side_sem.at[0]).start()
    send(kv_ref, rank, mate, core_sem.at[0]).start()
    own = pltpu.make_async_copy(kv_ref, kv_all.at[rank], own_sem.at[0])
    own.start()
    far_copy = pltpu.make_async_remote_copy(
        src_ref=q_ref.at[:, pl.ds(half, half)],
        dst_ref=q_far,
        send_sem=q_sem.at[0],
        recv_sem=q_sem.at[1],
        device_id={"ctx": far},
        device_id_type=MESH,
    )
    far_copy.start()

    def split_queries(source, g):
        for t in range(tiles):
            wide = source[:, t * HD : (t + 1) * HD].astype(jnp.float32) * scale
            high = wide.astype(jnp.bfloat16)
            q_two[g, t, :, :HD] = high
            q_two[g, t, :, HD:] = (wide - high.astype(jnp.float32)).astype(jnp.bfloat16)

    acc[...] = jnp.zeros_like(acc)
    total[...] = jnp.zeros_like(total)
    top[...] = jnp.full_like(top, NEG_FILL)
    split_queries(q_ref, 0)

    relay(0)
    arrived(other)
    send(kv_all.at[other], other, up, up_sem.at[1]).start()
    send(kv_all.at[other], other, down, down_sem.at[1]).start()
    send(kv_all.at[other], other, mate, core_sem.at[1]).start()
    own.wait()

    def slab_of(s):
        dist = (s + 1) // 2
        return jnp.where(s % 2 == 1, z + SLABS - dist, jnp.where(s == 7, z + 4, z + dist)) % SLABS

    def last_step(limit):
        last = 0
        for s in range(SLABS):
            last = jnp.where(slab_of(s) <= limit, s, last)
        return last

    last_own = last_step(z)
    last_far = last_step(SLABS - 1 - z)

    def body(slab, g, offset):
        keys = kv_all[pl.ds(slab * WIDE, WIDE), 0].reshape(WIDE * rows, HD)
        vals = kv_all[pl.ds(slab * WIDE, WIDE), 1].reshape(WIDE * rows, HD)
        keys = jnp.concatenate([keys, keys], axis=1)
        vals = jnp.concatenate([vals, jnp.ones_like(vals)], axis=1)
        scores = [
            lax.dot_general(
                q_two[g, t],
                keys,
                (((1,), (1,)), ((), ())),
                preferred_element_type=jnp.float32,
            )
            for t in range(tiles)
        ]
        if offset is not None:
            shape = (rows, WIDE * rows)
            ahead = lax.broadcasted_iota(jnp.int32, shape, 1) - lax.broadcasted_iota(
                jnp.int32, shape, 0
            )
            allowed = ahead <= offset
            scores = [jnp.where(allowed, s, NEG_FILL) for s in scores]
        for t in range(tiles):
            before = top[g, t]
            now = jnp.maximum(before, jnp.max(scores[t], axis=1, keepdims=True))
            weights = jnp.exp2(scores[t] - now[:, :1]).astype(jnp.bfloat16)
            fade = jnp.exp2(before - now)
            top[g, t] = now
            mixed = lax.dot_general(
                weights, vals, (((1,), (0,)), ((), ())), preferred_element_type=jnp.float32
            )
            acc[g, t] = acc[g, t] * fade + mixed[:, :HD]
            total[g, t] = total[g, t] * fade + mixed[:, HD:]

    def piece(g, hop, owner):
        peer = (head + hop) % heads_n
        column = pl.multiple_of(head * (2 * half) + g * half, half)
        return pltpu.make_async_remote_copy(
            src_ref=stage.at[g, pl.ds(peer * share, share)],
            dst_ref=out_ref.at[:, pl.ds(column, half)],
            send_sem=out_send.at[g, hop],
            recv_sem=out_recv.at[g, hop],
            device_id={"heads": peer, "ctx": owner},
            device_id_type=MESH,
        )

    def own_piece():
        column = pl.multiple_of(head * (2 * half), half)
        return pltpu.make_async_copy(
            stage.at[0, pl.ds(head * share, share)],
            out_ref.at[:, pl.ds(column, half)],
            own_sem.at[1],
        )

    def finish(g):
        for t in range(tiles):
            stage[g, :, t * HD : (t + 1) * HD] = (acc[g, t] / total[g, t]).astype(stage.dtype)

    def step(i, carry):
        s, g = i // 2, i % 2
        slab = slab_of(s)
        k = jnp.where(i == 1, 1, s + 1)

        @pl.when(jnp.logical_or(i == 1, jnp.logical_and(g == 0, jnp.logical_and(s >= 1, k < SEQ))))
        def _():
            relay(k)

        @pl.when(i == 1)
        def _():
            far_copy.wait_recv()
            split_queries(q_far, 1)

        @pl.when(g == 0)
        def _():
            for y in range(2):
                arrived(slab * WIDE + 2 * y + (1 - rank % 2))

        limit = jnp.where(g == 0, z, SLABS - 1 - z)
        owner = jnp.where(g == 0, rank, far)

        @pl.when(slab < limit)
        def _():
            body(slab, g, None)

        @pl.when(slab == limit)
        def _():
            body(slab, g, (owner % WIDE) * rows)

        @pl.when(jnp.logical_and(g == 0, s == last_own))
        def _():
            finish(0)
            for hop in range(1, heads_n):
                piece(0, hop, rank).start()
            own_piece().start()

        @pl.when(jnp.logical_and(g == 1, s == last_far))
        def _():
            finish(1)
            for hop in range(heads_n):
                piece(1, hop, far).start()

        return carry

    lax.fori_loop(0, 2 * SLABS, step, 0)

    own_piece().wait()
    for hop in range(heads_n):
        if hop:
            piece(0, hop, rank).wait_send()
            piece(0, hop, rank).wait_recv()
        piece(1, hop, far).wait_send()
        piece(1, hop, far).wait_recv()
    far_copy.wait_send()
    send(kv_ref, rank, other, side_sem.at[0]).wait_send()
    for n in range(2 + 2 * SEQ):
        send(kv_ref, rank, mate, core_sem.at[n]).wait_send()
    for n in (0, 1, 2, 3, 4, 5, 6):
        send(kv_ref, rank, up, up_sem.at[n]).wait_send()
    for n in (0, 1, 2, 3, 4, 6, 7):
        send(kv_ref, rank, down, down_sem.at[n]).wait_send()


def local(heads_n, queries, keys, values, positions):
    rows = queries.shape[0]
    group = queries.shape[1] // HD
    cosine, sine_table = rotary_tables(positions, HD)
    rot_q = rotate(queries.astype(jnp.float32).reshape(rows, group, HD), cosine, sine_table)
    rot_q = rot_q.astype(jnp.bfloat16).reshape(rows, group * HD)
    rot_k = rotate(keys.astype(jnp.float32).reshape(rows, 1, HD), cosine, sine_table)
    rot_k = rot_k.astype(jnp.bfloat16).reshape(rows, HD)
    both = jnp.stack([rot_k, values])
    tiles = group // 2
    ranks = SLABS * WIDE
    vmem = pl.BlockSpec(memory_space=pltpu.VMEM)
    dma = pltpu.SemaphoreType.DMA
    return pl.pallas_call(
        functools.partial(attend_kernel, heads_n),
        out_shape=jax.ShapeDtypeStruct((rows // heads_n, heads_n * group * HD), jnp.bfloat16),
        in_specs=[vmem, vmem],
        out_specs=vmem,
        scratch_shapes=[
            pltpu.VMEM((ranks, 2, rows, HD), jnp.bfloat16),
            pltpu.VMEM((rows, tiles * HD), jnp.bfloat16),
            pltpu.VMEM((2, tiles, rows, 2 * HD), jnp.bfloat16),
            pltpu.VMEM((2, tiles, rows, HD), jnp.float32),
            pltpu.VMEM((2, tiles, rows, HD), jnp.float32),
            pltpu.VMEM((2, tiles, rows, HD), jnp.float32),
            pltpu.VMEM((2, rows, tiles * HD), jnp.bfloat16),
            dma((2,)),
            dma((1,)),
            dma((ranks,)),
            dma((SEQ + 2,)),
            dma((SEQ + 2,)),
            dma((2 + 2 * SEQ,)),
            dma((2,)),
            dma((2, heads_n)),
            dma((2, heads_n)),
        ],
        compiler_params=pltpu.CompilerParams(
            collective_id=0, has_side_effects=True, vmem_limit_bytes=60000 * 1024
        ),
    )(rot_q, both)


def solution(mesh):
    return jax.shard_map(
        functools.partial(local, mesh.shape["heads"]),
        mesh=mesh,
        in_specs=(P("ctx", "heads"), P("ctx", "heads"), P("ctx", "heads"), P("ctx")),
        out_specs=P(("ctx", "heads"), None),
        check_vma=False,
    )
```

```python
import functools
import math

import jax
import jax.numpy as jnp
from jax import lax
from jax.experimental import pallas as pl
from jax.experimental.pallas import tpu as pltpu
from jax.sharding import PartitionSpec as P

HD = 128
NEG_FILL = -1e30
MESH = pl.DeviceIdType.MESH
SLABS = 8
WIDE = 4
LINE = 5


def rotary_tables(positions, head_dim):
    step_index = jnp.arange(head_dim // 2, dtype=jnp.float32)
    base_freq = jnp.power(jnp.float32(500000.0), -(2.0 * step_index / head_dim))
    wavelen = 2.0 * math.pi / base_freq
    blend_factor = (8192.0 / wavelen - 1.0) / 3.0
    middle = (1.0 - blend_factor) * base_freq / 8.0 + blend_factor * base_freq
    inv_freq = jnp.where(
        wavelen < 2048.0, base_freq, jnp.where(wavelen > 8192.0, base_freq / 8.0, middle)
    )
    angles = positions.astype(jnp.float32)[:, None] * inv_freq[None, :]
    return (jnp.cos(angles), jnp.sin(angles))


def attend_kernel(
    heads_n,
    q_ref,
    k_ref,
    v_ref,
    cos_ref,
    sin_ref,
    out_ref,
    kv_all,
    q_move,
    q_far,
    q_two,
    acc,
    total,
    top,
    stage,
    own_sem,
    recv_sem,
    up_sem,
    down_sem,
    side_sem,
    core_sem,
    q_send,
    q_recv,
    out_send,
    out_recv,
):
    rows = q_ref.shape[0]
    pair = 2 * HD
    pairs = q_ref.shape[1] // pair
    share = rows // heads_n
    scale = math.log2(math.e) / math.sqrt(HD)
    head = lax.axis_index("heads")
    rank = lax.axis_index("ctx")
    ranks = SLABS * WIDE
    z = rank // WIDE
    place = rank % WIDE
    across = (place + 2) % WIDE
    mate = rank + 1 - 2 * (rank % 2)
    other = z * WIDE + across
    up = (rank + WIDE) % ranks
    down = (rank + ranks - WIDE) % ranks
    helper = z == 0
    giver = z >= SLABS - 2
    sources = tuple((SLABS - 1 - n) * WIDE + place for n in range(2))

    def turn(x):
        wide = x.astype(jnp.float32)
        turned = wide * cos_ref[...] + pltpu.roll(wide, HD // 2, axis=1) * sin_ref[...]
        return turned.astype(jnp.bfloat16)

    kv_all[rank, 0] = turn(k_ref[...])
    kv_all[rank, 1] = v_ref[...]
    for t in range(2):
        column = (2 * pairs - 2 + t) * HD
        q_move[:, t * HD : (t + 1) * HD] = turn(q_ref[:, column : column + HD])

    barrier = pltpu.get_barrier_semaphore()
    for peer in (mate, other, up, down):
        pl.semaphore_signal(barrier, inc=1, device_id={"ctx": peer}, device_id_type=MESH)
    for hop in range(1, heads_n):
        peer = (head + hop) % heads_n
        pl.semaphore_signal(
            barrier, inc=1, device_id={"heads": peer, "ctx": rank}, device_id_type=MESH
        )

    def greet(ctx):
        for hop in range(heads_n):
            peer = (head + hop) % heads_n
            pl.semaphore_signal(
                barrier, inc=1, device_id={"heads": peer, "ctx": ctx}, device_id_type=MESH
            )

    @pl.when(helper)
    def _():
        for source in sources:
            greet(source)

    @pl.when(giver)
    def _():
        greet(place)

    more = jnp.where(helper, 2 * heads_n, jnp.where(giver, heads_n, 0))
    pl.semaphore_wait(barrier, 3 + heads_n + more)

    def send(source, slot, peer, sem):
        return pltpu.make_async_remote_copy(
            src_ref=source,
            dst_ref=kv_all.at[slot],
            send_sem=sem,
            recv_sem=recv_sem.at[slot],
            device_id={"ctx": peer},
            device_id_type=MESH,
        )

    def arrived(slot):
        send(kv_all.at[slot], slot, mate, core_sem.at[0]).wait_recv()

    def slot_at(shift, mine):
        return ((z + shift + SLABS) % SLABS) * WIDE + (place if mine else across)

    peers = {"up": (up, up_sem), "down": (down, down_sem), "side": (other, side_sem)}

    def relay(shift, mine, core_at, *onward):
        slot = slot_at(shift, mine)
        arrived(slot)
        for way, at in onward:
            peer, sem = peers[way]
            send(kv_all.at[slot], slot, peer, sem.at[at]).start()
        send(kv_all.at[slot], slot, mate, core_sem.at[core_at]).start()

    def event(n):
        if n == 0:
            relay(-1, True, 1, ("up", 1), ("side", 1))
            relay(1, True, 2, ("down", 1), ("side", 2))
            relay(0, False, 3)
        elif n == 1:
            relay(-2, True, 4, ("up", 2))
            relay(2, True, 5, ("down", 2))
            relay(-1, False, 6, ("up", 3))
        elif n == 2:
            relay(-3, True, 7, ("up", 4), ("side", 3))
            relay(3, True, 8)
            relay(1, False, 9, ("down", 3))
        elif n == 3:
            relay(2, False, 10, ("down", 4))
            relay(-2, False, 11)
        elif n == 4:
            relay(-4, True, 12, ("side", 4))
            relay(3, False, 13)
            relay(-3, False, 14)
        else:
            relay(-4, False, 15)

    mine = kv_all.at[rank]
    send(mine, rank, other, side_sem.at[0]).start()
    send(mine, rank, up, up_sem.at[0]).start()
    send(mine, rank, down, down_sem.at[0]).start()
    send(mine, rank, mate, core_sem.at[0]).start()

    def far_copy(n):
        return pltpu.make_async_remote_copy(
            src_ref=q_move,
            dst_ref=q_far.at[n],
            send_sem=q_send.at[n],
            recv_sem=q_recv.at[n],
            device_id={"ctx": place},
            device_id_type=MESH,
        )

    for n in range(2):

        @pl.when(z == SLABS - 1 - n)
        def _():
            far_copy(n).start()

    def split_queries(turned, at):
        wide = turned.astype(jnp.float32) * scale
        high = wide.astype(jnp.bfloat16)
        q_two[at, :, :HD] = high
        q_two[at, :, HD:] = (wide - high.astype(jnp.float32)).astype(jnp.bfloat16)

    acc[...] = jnp.zeros_like(acc)
    total[...] = jnp.zeros_like(total)
    top[...] = jnp.full_like(top, NEG_FILL)
    for t in range(2 * pairs):
        split_queries(turn(q_ref[:, t * HD : (t + 1) * HD]), t)

    def slab_of(s):
        n = jnp.maximum(s - 1, 0)
        dist = (n + 1) // 2
        return jnp.where(n % 2 == 1, z + SLABS - dist, jnp.where(n == 7, z + 4, z + dist)) % SLABS

    def last_step(limit):
        last = 1
        for s in range(2, SLABS + 1):
            last = jnp.where(slab_of(s) <= limit, s, last)
        return last

    lasts = (last_step(z), last_step(SLABS - 1), last_step(SLABS - 2))

    def body(first, width, base, tiles, offset):
        keys = kv_all[pl.ds(first, width), 0].reshape(width * rows, HD)
        vals = kv_all[pl.ds(first, width), 1].reshape(width * rows, HD)
        keys = jnp.concatenate([keys, keys], axis=1)
        vals = jnp.concatenate([vals, jnp.ones_like(vals)], axis=1)
        scores = [
            lax.dot_general(
                q_two[base + t],
                keys,
                (((1,), (1,)), ((), ())),
                preferred_element_type=jnp.float32,
            )
            for t in range(tiles)
        ]
        if offset is not None:
            shape = (rows, width * rows)
            ahead = lax.broadcasted_iota(jnp.int32, shape, 1) - lax.broadcasted_iota(
                jnp.int32, shape, 0
            )
            allowed = ahead <= offset
            scores = [jnp.where(allowed, s, NEG_FILL) for s in scores]
        for t in range(tiles):
            before = top[base + t]
            now = jnp.maximum(before, jnp.max(scores[t], axis=1, keepdims=True))
            weights = jnp.exp2(scores[t] - now[:, :1]).astype(jnp.bfloat16)
            fade = jnp.exp2(before - now)
            top[base + t] = now
            mixed = lax.dot_general(
                weights, vals, (((1,), (0,)), ((), ())), preferred_element_type=jnp.float32
            )
            acc[base + t] = acc[base + t] * fade + mixed[:, :HD]
            total[base + t] = total[base + t] * fade + mixed[:, HD:]

    def out_columns(p):
        return pl.ds(pl.multiple_of((head * pairs + p) * pair, pair), pair)

    def piece(at, p, hop, owner):
        peer = (head + hop) % heads_n
        return pltpu.make_async_remote_copy(
            src_ref=stage.at[at, pl.ds(peer * share, share)],
            dst_ref=out_ref.at[:, out_columns(p)],
            send_sem=out_send.at[at, hop],
            recv_sem=out_recv.at[p, hop],
            device_id={"heads": peer, "ctx": owner},
            device_id_type=MESH,
        )

    def own_piece(p):
        return pltpu.make_async_copy(
            stage.at[p, pl.ds(head * share, share)],
            out_ref.at[:, out_columns(p)],
            own_sem.at[p],
        )

    def finish(at):
        for t in range(2):
            tile = acc[2 * at + t] / total[2 * at + t]
            stage[at, :, t * HD : (t + 1) * HD] = tile.astype(stage.dtype)
        if at < pairs:
            for hop in range(1, heads_n):
                piece(at, at, hop, rank).start()
            own_piece(at).start()
        else:
            for hop in range(heads_n):
                piece(at, pairs - 1, hop, sources[at - pairs]).start()

    kept = jnp.where(giver, pairs - 1, pairs)

    def step(i, carry):
        s, item = i // 4, i % 4
        slab = slab_of(s)
        for n in range(6):

            @pl.when(i == (4, 5, 9, 13, 17, 21)[n])
            def _():
                event(n)

        @pl.when(jnp.logical_and(i == 6, helper))
        def _():
            for n in range(2):
                far_copy(n).wait_recv()
                for t in range(2):
                    split_queries(q_far[n, :, t * HD : (t + 1) * HD], 2 * (pairs + n) + t)

        @pl.when(i == 0)
        def _():
            arrived(mate)

        @pl.when(i == 4)
        def _():
            arrived(z * WIDE + 2 * (1 - place // 2) + 1 - place % 2)

        @pl.when(jnp.logical_and(s >= 2, item == 0))
        def _():
            for y in range(2):
                arrived(slab * WIDE + 2 * y + (1 - place % 2))

        limit = jnp.where(item == 2, SLABS - 1, jnp.where(item == 3, SLABS - 2, z))
        count = jnp.where(
            item >= 2, jnp.where(helper, 1, 0), jnp.where(jnp.logical_and(item == 1, giver), 1, 2)
        )
        base = jnp.where(item >= 2, 2 * item + 4, 4 * item)
        whole = jnp.logical_and(slab < limit, s >= 1)
        edge = slab == limit
        first = slab * WIDE

        for n in (2, 1):

            @pl.when(jnp.logical_and(count == n, whole))
            def _():
                body(first, WIDE, base, 2 * n, None)

            @pl.when(jnp.logical_and(count == n, jnp.logical_and(edge, s != 1)))
            def _():
                body(first + 2 * (place // 2), 2, base, 2 * n, (place % 2) * rows)

            low = jnp.logical_and(edge, jnp.logical_and(s != 0, place >= 2))

            @pl.when(jnp.logical_and(count == n, low))
            def _():
                body(first, 2, base, 2 * n, None)

        done = s == jnp.where(item == 2, lasts[1], jnp.where(item == 3, lasts[2], lasts[0]))
        for at, its, need in ((0, 0, 1), (1, 0, 2), (2, 1, 1), (3, 1, 2), (4, 2, 1), (5, 3, 1)):

            @pl.when(jnp.logical_and(done, jnp.logical_and(item == its, count >= need)))
            def _():
                finish(at)

        return carry

    lax.fori_loop(0, 4 * (SLABS + 1), step, 0)

    for p in range(pairs):

        @pl.when(kept > p)
        def _():
            own_piece(p).wait()
            for hop in range(1, heads_n):
                piece(p, p, hop, rank).wait_send()

        @pl.when(kept <= p)
        def _():
            piece(p, p, 0, rank).wait_recv()

        for hop in range(1, heads_n):
            piece(p, p, hop, rank).wait_recv()
    for n in range(2):

        @pl.when(helper)
        def _():
            for hop in range(heads_n):
                piece(pairs + n, pairs - 1, hop, sources[n]).wait_send()

        @pl.when(z == SLABS - 1 - n)
        def _():
            far_copy(n).wait_send()

    for n in range(2 * SLABS):
        send(mine, rank, mate, core_sem.at[n]).wait_send()
    for n in range(LINE):
        send(mine, rank, up, up_sem.at[n]).wait_send()
        send(mine, rank, down, down_sem.at[n]).wait_send()
        send(mine, rank, other, side_sem.at[n]).wait_send()


def local(heads_n, queries, keys, values, positions):
    rows = queries.shape[0]
    group = queries.shape[1] // HD
    cosine, sine_table = rotary_tables(positions, HD)
    cosines = jnp.concatenate([cosine, cosine], axis=1)
    sines = jnp.concatenate([-sine_table, sine_table], axis=1)
    tiles = group + group // 2
    ranks = SLABS * WIDE
    vmem = pl.BlockSpec(memory_space=pltpu.VMEM)
    dma = pltpu.SemaphoreType.DMA
    return pl.pallas_call(
        functools.partial(attend_kernel, heads_n),
        out_shape=jax.ShapeDtypeStruct((rows // heads_n, heads_n * group * HD), jnp.bfloat16),
        in_specs=[vmem] * 5,
        out_specs=vmem,
        scratch_shapes=[
            pltpu.VMEM((ranks, 2, rows, HD), jnp.bfloat16),
            pltpu.VMEM((rows, 2 * HD), jnp.bfloat16),
            pltpu.VMEM((2, rows, 2 * HD), jnp.bfloat16),
            pltpu.VMEM((tiles, rows, 2 * HD), jnp.bfloat16),
            pltpu.VMEM((tiles, rows, HD), jnp.float32),
            pltpu.VMEM((tiles, rows, HD), jnp.float32),
            pltpu.VMEM((tiles, rows, HD), jnp.float32),
            pltpu.VMEM((tiles // 2, rows, 2 * HD), jnp.bfloat16),
            dma((group // 2,)),
            dma((ranks,)),
            dma((LINE,)),
            dma((LINE,)),
            dma((LINE,)),
            dma((2 * SLABS,)),
            dma((2,)),
            dma((2,)),
            dma((tiles // 2, heads_n)),
            dma((group // 2, heads_n)),
        ],
        compiler_params=pltpu.CompilerParams(
            collective_id=0, has_side_effects=True, vmem_limit_bytes=60000 * 1024
        ),
    )(queries, keys, values, cosines, sines)


def solution(mesh):
    return jax.shard_map(
        functools.partial(local, mesh.shape["heads"]),
        mesh=mesh,
        in_specs=(P("ctx", "heads"), P("ctx", "heads"), P("ctx", "heads"), P("ctx")),
        out_specs=P(("ctx", "heads"), None),
        check_vma=False,
    )
```
